32 devices in a mesh: grp: 4 (over y, x), row: 2 (over core), col: 4 (over z).
Axes of the slice: x: 2, y: 2, z: 4, core: 2. Of those that a mesh axis runs over, the one named last changes fastest.
Arguments:
- normals: float32 [4, 4096, 4096], P('grp', 'row', 'col'), as said below
- transforms: float32 [4, 32, 128, 128], P('grp', 'row'), as said below
- block_map: int32 [4, 32], P('grp'), may hold values from 0 to 31, as said below
Outputs:
- eliminated: float32 [4096, 4096], P('row', 'col')
The draws below stay inside these ranges and needn't reach their ends.
Inputs may be any that keep to these rules, and one draw needn't show every extreme that they name: `block_map`: for each group, a permutation of the blocks that maps every aligned range of 8 blocks onto itself. `normals`: each group's matrix is symmetric positive definite. `transforms`: each block is nonsingular.
All inputs are finite; a program needn't handle non-finite values.
Results may differ from the reference program's by a relative error of at most 0.0001.
Values sent between devices are 32-bit elements; how exact they have to be, the bound alone decides.
No kernel may reach another device: no remote copies, remote signals or barrier semaphores. Data moves between devices by JAX's collectives and lax.ppermute only.
A program may use at most 64 MiB of HBM per device.

```python
import jax
import jax.numpy as jnp
from jax import lax

P_SIZE = 4096
BLK = 128
NPAN = 5
GROUPS = 4
NB = 32
SPAN = 8


loading_count = 64


def draw_normals(key, part):
    key_noise = jax.random.fold_in(key, 0)
    key_scale = jax.random.fold_in(key, 1)
    key_loading = jax.random.fold_in(key, 3)
    noise_field = jax.random.normal(key_noise, (GROUPS, P_SIZE, P_SIZE), jnp.float32)
    scales = jnp.exp(jax.random.uniform(key_scale, (GROUPS, P_SIZE), jnp.float32, jnp.log(0.3), jnp.log(3.0)))
    loadings = jax.random.normal(key_loading, (GROUPS, P_SIZE, loading_count), jnp.float32)
    loadings = loadings * jnp.sqrt(3.0 / loading_count)
    shared = jnp.einsum('gpr,gqr->gpq', loadings, loadings, precision=lax.Precision.HIGHEST)
    symmetric = (noise_field + jnp.swapaxes(noise_field, 1, 2)) / jnp.sqrt(2.0 * P_SIZE)
    base_core = symmetric + shared + 3.0 * jnp.eye(P_SIZE, dtype=jnp.float32)[None]
    return scales[:, :, None] * base_core * scales[:, None, :] / GROUPS


def draw_transforms(key, part):
    noise_blocks = jax.random.normal(key, (GROUPS, NB, BLK, BLK), jnp.float32)
    return jnp.eye(BLK, dtype=jnp.float32)[None, None] + 0.5 / jnp.sqrt(1.0 * BLK) * noise_blocks


def draw_block_map(key, part):
    sort_scores = jax.random.randint(key, (GROUPS, NB // SPAN, SPAN), 0, 2 ** 20)
    sort_scores = sort_scores * SPAN + jnp.arange(SPAN, dtype=jnp.int32)[None, None, :]
    block_order = jnp.argsort(sort_scores, axis=2, stable=True).astype(jnp.int32)
    range_starts = (jnp.arange(NB // SPAN, dtype=jnp.int32) * SPAN)[None, :, None]
    return (block_order + range_starts).reshape(GROUPS, NB)


def setup_inputs(seed: int = 0) -> dict:
    arg_keys = jax.random.split(jax.random.key(seed), 4)
    return {
        "normals": draw_normals(jax.random.fold_in(arg_keys[3], 71), 0),
        "transforms": draw_transforms(jax.random.fold_in(arg_keys[3], 71), 0),
        "block_map": draw_block_map(jax.random.fold_in(arg_keys[3], 71), 0),
    }


def transform_group(normal, blocks, mapping):
    nblocks = P_SIZE // BLK
    grid = normal.reshape(nblocks, BLK, nblocks, BLK)
    half_done = jnp.einsum('aij,aibk->ajbk', blocks, grid, precision=lax.Precision.HIGHEST)
    rotated = jnp.einsum('ajbk,bkl->ajbl', half_done, blocks, precision=lax.Precision.HIGHEST)
    rotated = jnp.take(rotated, mapping.astype(jnp.int32), axis=0)
    rotated = jnp.take(rotated, mapping.astype(jnp.int32), axis=2)
    return rotated.reshape(P_SIZE, P_SIZE)

def reference(normals, transforms, block_map):

    def add_group(group, combined):
        return combined + transform_group(normals[group], transforms[group], block_map[group])
    matrix = lax.fori_loop(0, GROUPS, add_group, jnp.zeros((P_SIZE, P_SIZE), jnp.float32))
    for panel in range(NPAN):
        offset = panel * BLK
        column = matrix[:, offset:offset + BLK]
        factor_block = jnp.linalg.cholesky(column[offset:offset + BLK])
        factor = lax.linalg.triangular_solve(factor_block, column, left_side=False, lower=True, transpose_a=True)
        below = jnp.arange(P_SIZE)[:, None] >= offset
        factor = jnp.where(below, factor, jnp.zeros_like(factor))
        matrix = matrix - jnp.dot(factor.astype(jnp.float32), factor.T.astype(jnp.float32), precision=lax.Precision.HIGHEST, preferred_element_type=jnp.float32)
        matrix = matrix.at[:, offset:offset + BLK].set(factor)
    return matrix
```

```python
import functools

import jax
import jax.numpy as jnp
import numpy as np
from jax import lax
from jax.experimental import pallas as pl
from jax.experimental.pallas import tpu as pltpu
from jax.sharding import PartitionSpec as P

BLK = 128
NPAN = 5
NEAR, FAR = 1, 2
ALL = ("grp", "row", "col")


def spread(block, axis, holder):
    block = jnp.where(lax.axis_index(axis) == holder, block, jnp.zeros_like(block))
    return lax.psum(block, axis)


def general(normals, transforms, block_map):
    local = normals[0]
    height, width = local.shape
    row_blocks = height // BLK
    col_blocks = width // BLK
    row_index = lax.axis_index("row")
    col_index = lax.axis_index("col")
    row_transforms = transforms[0]
    every_block = lax.all_gather(transforms, "row", axis=1, tiled=True)[0]
    col_transforms = lax.dynamic_slice_in_dim(every_block, col_index * col_blocks, col_blocks, 0)
    grid = local.reshape(row_blocks, BLK, col_blocks, BLK)
    half_done = jnp.einsum("aij,aibk->ajbk", row_transforms, grid, precision=lax.Precision.HIGHEST)
    rotated = jnp.einsum(
        "ajbk,bkl->ajbl", half_done, col_transforms, precision=lax.Precision.HIGHEST
    )
    mapping = block_map[0]
    row_map = (
        lax.dynamic_slice_in_dim(mapping, row_index * row_blocks, row_blocks, 0)
        - row_index * row_blocks
    )
    col_map = (
        lax.dynamic_slice_in_dim(mapping, col_index * col_blocks, col_blocks, 0)
        - col_index * col_blocks
    )
    rotated = jnp.take(rotated, row_map, axis=0)
    rotated = jnp.take(rotated, col_map, axis=2).reshape(height, width)
    matrix = lax.psum(rotated, "grp")
    row_offset = row_index * height
    own_count = matrix.shape[0]
    order_all = height * lax.axis_size("row")
    col_offset = col_index * width
    for panel in range(NPAN):
        offset = panel * BLK
        holder = offset // width
        inside = offset - holder * width
        panel_piece = spread(matrix[:, inside : inside + BLK], "col", holder)
        column = lax.all_gather(panel_piece, "row", axis=0, tiled=True)
        factor_block = jnp.linalg.cholesky(column[offset : offset + BLK])
        factor = lax.linalg.triangular_solve(
            factor_block, column, left_side=False, lower=True, transpose_a=True
        )
        below = jnp.arange(order_all)[:, None] >= offset
        factor = jnp.where(below, factor, jnp.zeros_like(factor))
        own_rows = lax.dynamic_slice_in_dim(factor, row_offset, own_count, 0)
        col_rows = lax.dynamic_slice_in_dim(factor, col_offset, width, 0)
        matrix = matrix - jnp.dot(
            own_rows,
            col_rows.T,
            precision=lax.Precision.HIGHEST,
            preferred_element_type=jnp.float32,
        )
        current = matrix[:, inside : inside + BLK]
        matrix = matrix.at[:, inside : inside + BLK].set(
            jnp.where(col_index == holder, own_rows, current)
        )
    return matrix


class Plan:
    def __init__(self, R, C, rb, cb):
        self.R, self.C, self.rb, self.cb = R, C, rb, cb
        self.T = [(a, b) for b in range(NPAN) for a in range(b, NPAN)]
        self.strips = [
            [(i, 2 * q + s) for q in range(4) for i in range(NPAN)] for s in range(2)
        ]
        inner = lambda c, low: [
            (a, b)
            for a in range(c * cb, (c + 1) * cb)
            for b in range(c * cb, a + 1)
            if b >= low
        ]
        box = lambda rows, cols: [(a, b) for a in rows for b in cols if a >= NPAN and b >= NPAN]
        rng = lambda c: range(c * cb, (c + 1) * cb)
        half = cb // 2
        top = lambda c: range(c * cb, c * cb + half)
        bot = lambda c: range(c * cb + half, (c + 1) * cb)
        first, second, stay = {}, {}, {}
        first[0, 0] = box(rng(1), rng(0))
        stay[0, 0] = inner(0, NPAN)
        first[0, 1] = []
        stay[0, 1] = inner(1, 0)
        first[0, 2] = [(b, a) for a, b in box(bot(2), rng(1))]
        first[0, 3] = [(b, a) for a, b in box(bot(3), rng(1))]
        first[1, 0] = box(rng(2), rng(0))
        second[1, 0] = box(rng(3), rng(0))
        first[1, 1] = box(top(3), rng(1))
        second[1, 1] = box(top(2), rng(1))
        first[1, 2] = []
        stay[1, 2] = inner(2, 0)
        second[1, 2] = box(top(3), rng(2))
        first[1, 3] = []
        stay[1, 3] = inner(3, 0)
        second[1, 3] = [(b, a) for a, b in box(bot(3), rng(2))]
        self.na, self.nb = 9, 8
        self.sent = 8
        self.A = self.fill(first, stay, self.na)
        self.B = self.fill(second, {}, self.nb)
        self.e1 = [((0, 0), (0, 1)), ((0, 2), (1, 1)), ((1, 0), (0, 2)), ((1, 1), (0, 3))]
        self.e2 = [
            ((1, 2), (1, 3)),
            ((1, 3), (1, 2)),
            ((1, 1), (0, 2)),
            ((1, 0), (0, 3)),
            ((0, 3), (1, 1)),
        ]
        self.check()

    def fill(self, sends, stays, n):
        out = {}
        for r in range(self.R):
            for c in range(self.C):
                slots = [[None] * n for _ in range(4)]
                send = list(sends.get((r, c), []))
                per = -(-len(send) // 4)
                for q in range(4):
                    for i, blk in enumerate(send[q * per : (q + 1) * per]):
                        slots[q][i] = blk
                rest = list(stays.get((r, c), []))
                for q in range(4):
                    for i in range(n):
                        if slots[q][i] is None and rest:
                            slots[q][i] = rest.pop()
                assert not rest
                out[r, c] = slots
        return out

    def owner_tables(self, slots, n):
        t = np.zeros((6, self.R * self.C, 4 * n), np.int32)
        t[2:] = -1
        for (r, c), qs in slots.items():
            d = r * self.C + c
            for q in range(4):
                for i in range(n):
                    if qs[q][i] is None:
                        continue
                    a, b = qs[q][i]
                    la, lb = a - r * self.rb, b - c * self.cb
                    assert 0 <= la < self.rb and 0 <= lb < self.cb
                    t[:4, d, q * n + i] = la, lb, la, lb
                    ta, tb = b - r * self.rb, a - c * self.cb
                    if a != b and 0 <= ta < self.rb and 0 <= tb < self.cb:
                        t[4:, d, q * n + i] = ta, tb
        return t

    def partner_tables(self, edges, n):
        t = np.full((6, self.R * self.C, 4 * n), -1, np.int32)
        for src, (r, c) in edges:
            slots = self.source(edges, src)
            d = r * self.C + c
            for q in range(4):
                for i in range(n):
                    if slots[src][q][i] is None:
                        continue
                    a, b = slots[src][q][i]
                    ta, tb = b - r * self.rb, a - c * self.cb
                    if 0 <= ta < self.rb and 0 <= tb < self.cb:
                        t[4:, d, q * n + i] = ta, tb
        return t

    def source(self, edges, src):
        return self.A if edges is self.e1 or src == (0, 3) else self.B

    def check(self):
        tabs = [
            self.owner_tables(self.A, self.na),
            self.owner_tables(self.B, self.nb),
            self.partner_tables(self.e1, self.sent),
            self.partner_tables(self.e2, self.sent),
        ]
        for r in range(self.R):
            for c in range(self.C):
                d = r * self.C + c
                hits = np.zeros((self.rb, self.cb), np.int32)
                for t in tabs:
                    for s in range(t.shape[2]):
                        for k in (2, 4):
                            if t[k, d, s] >= 0:
                                hits[t[k, d, s], t[k + 1, d, s]] += 1
                for a in range(self.rb):
                    for b in range(self.cb):
                        panel = a + r * self.rb < NPAN or b + c * self.cb < NPAN
                        assert hits[a, b] == (0 if panel else 1), (r, c, a, b)


@functools.lru_cache(maxsize=None)
def plan_for(R, C, rb, cb):
    return Plan(R, C, rb, cb)


def fits(mesh):
    shape = dict(mesh.shape)
    return shape["grp"] == 4 and shape["row"] == 2 and shape["col"] == 4


f32, bf16 = jnp.float32, jnp.bfloat16


def halves(x):
    high = x.astype(bf16)
    return high, (x - high.astype(f32)).astype(bf16)


def dot3(a, b, ka, kb):
    ah, al = a if isinstance(a, tuple) else halves(a)
    bh, bl = b if isinstance(b, tuple) else halves(b)
    left = jnp.concatenate([ah, ah, al], axis=ka)
    right = jnp.concatenate([bh, bl, bh], axis=kb)
    return lax.dot_general(
        left, right, (((ka,), (kb,)), ((), ())), preferred_element_type=f32
    )


def exact(a, b, ka, kb):
    return lax.dot_general(
        a, b, (((ka,), (kb,)), ((), ())),
        precision=lax.Precision.HIGHEST, preferred_element_type=f32,
    )


def place():
    return lax.axis_index("grp"), lax.axis_index("row"), lax.axis_index("col")


def transform_kernel(groups, active, rb, cb, C, tab, bmap, n_ref, hr, hc, *rest):
    outs = rest[:-2]
    nbuf, sems = rest[-2:]
    g, r, c = place()
    dev = r * C + c

    def source(k, n, i):
        base = 0 if k is None else (g ^ k) * n
        a = tab[0, dev, base + i]
        b = tab[1, dev, base + i]
        row = bmap[0, r * rb + a] - r * rb
        col = bmap[0, c * cb + b] - c * cb
        return row, col

    def copy(row, col, slot):
        return pltpu.make_async_copy(
            n_ref.at[pl.ds(pl.multiple_of(row * BLK, BLK), BLK),
                     pl.ds(pl.multiple_of(col * BLK, BLK), BLK)],
            nbuf.at[slot],
            sems.at[slot],
        )

    def run():
        slot0 = 0
        for _, _, n, k in groups:
            def start(i, carry, n=n, k=k, slot0=slot0):
                row, col = source(k, n, i)
                copy(row, col, slot0 + i).start()
                return carry
            lax.fori_loop(0, n, start, 0)
            slot0 += n
        slot0 = 0
        for o, lead, n, k in groups:
            out = outs[o]
            def work(i, carry, n=n, k=k, slot0=slot0, out=out, lead=lead):
                row, col = source(k, n, i)
                copy(row, col, slot0 + i).wait()
                half = dot3(hr[row], nbuf[slot0 + i], 0, 0)
                whole = dot3(half, hc[col], 1, 0)
                if lead is None:
                    out[i] = whole
                else:
                    out[lead, i] = whole
                return carry
            lax.fori_loop(0, n, work, 0, unroll=n if n < 6 else (n // 2 if n % 2 == 0 else n // 3))
            slot0 += n

    if active is None:
        run()
    else:
        pl.when(active(r, c))(run)


def transform(local, hr, hc, bmap, tab, shapes, groups, active, rb, cb, C):
    total = sum(n for _, _, n, _ in groups)
    smem = pl.BlockSpec(memory_space=pltpu.SMEM)
    vmem = pl.BlockSpec(memory_space=pltpu.VMEM)
    return pl.pallas_call(
        functools.partial(transform_kernel, groups, active, rb, cb, C),
        out_shape=[jax.ShapeDtypeStruct(s, f32) for s in shapes],
        in_specs=[smem, smem, pl.BlockSpec(memory_space=pl.ANY), vmem, vmem],
        out_specs=[vmem for _ in shapes],
        scratch_shapes=[
            pltpu.VMEM((total, BLK, BLK), f32),
            pltpu.SemaphoreType.DMA((total,)),
        ],
    )(tab, bmap, local, hr, hc)


def factor_block(a):
    lane = lax.broadcasted_iota(jnp.int32, (8, BLK), 1)
    sub = lax.broadcasted_iota(jnp.int32, (8, BLK), 0)
    eye = (
        lax.broadcasted_iota(jnp.int32, (BLK, BLK), 0)
        == lax.broadcasted_iota(jnp.int32, (BLK, BLK), 1)
    ).astype(f32)
    inv_rows = []
    rest_a, rest_w = a, eye
    for b in range(BLK // 8):
        ra = rest_a[0:8]
        rw = rest_w[0:8]
        for j in range(8):
            spot = b * 8 + j
            column = jnp.broadcast_to(ra[:, spot : spot + 1], (8, BLK))
            scale = lax.rsqrt(column[j : j + 1])
            row_a = ra[j : j + 1] * scale
            row_w = rw[j : j + 1] * scale
            mult = jnp.where(sub > j, column * scale, 0.0)
            here = sub == j
            ra = jnp.where(here, row_a, ra - mult * row_a)
            rw = jnp.where(here, row_w, rw - mult * row_w)
        inv_rows.append(rw)
        if b < BLK // 8 - 1:
            low = ra[:, (b + 1) * 8 :]
            rest_a = rest_a[8:] - exact(low, ra, 0, 0)
            rest_w = rest_w[8:] - exact(low, rw, 0, 0)
    return jnp.concatenate(inv_rows, axis=0)


def slot_of(a, b):
    return sum(NPAN - t for t in range(b)) + a - b


def factor_kernel(t_ref, l_ref):
    l_ref[...] = t_ref[...]
    for k in range(NPAN):
        inv = factor_block(l_ref[slot_of(k, k)])
        l_ref[slot_of(k, k)] = inv
        for i in range(k + 1, NPAN):
            l_ref[slot_of(i, k)] = exact(l_ref[slot_of(i, k)], inv, 1, 1)
        for j in range(k + 1, NPAN):
            for i in range(j, NPAN):
                l_ref[slot_of(i, j)] = l_ref[slot_of(i, j)] - exact(
                    l_ref[slot_of(i, k)], l_ref[slot_of(j, k)], 1, 1
                )


def factor_all(t):
    vmem = pl.BlockSpec(memory_space=pltpu.VMEM)
    return pl.pallas_call(
        factor_kernel,
        out_shape=jax.ShapeDtypeStruct(t.shape, f32),
        in_specs=[vmem],
        out_specs=vmem,
    )(t)


TILE = 256
WIDE = 512


def update_kernel(R, C, height, width, l_ref, *rest):
    sets = [rest[2 * i : 2 * i + 2] for i in range(6)]
    out_ref, xr, xc, raw, xch, xcl, sems = rest[12:]
    step = pl.program_id(0)
    g, r, c = place()
    depth = NPAN * BLK

    def pieces(pair, dst, offset, sem):
        got = []
        for s in range(2):
            for q in range(4):
                at = offset + (2 * q + s) * BLK
                got.append(
                    pltpu.make_async_copy(
                        pair[s].at[g ^ q], dst.at[:, pl.ds(at, BLK)], sems.at[sem, 4 * s + q]
                    )
                )
        return got

    @pl.when(step == 0)
    def _():
        own, swapped, b1, b2, c1, c2 = sets
        fixed = pieces(own, xc, 0, 2) + pieces(own, raw, 0, 3)
        for cp in fixed:
            cp.start()
        choice = {
            (0, 0): (own, swapped), (0, 1): (swapped, own), (0, 2): (b2, b1), (0, 3): (c2, c1),
            (1, 0): (c1, c2), (1, 1): (b1, b2), (1, 2): (own, swapped), (1, 3): (swapped, own),
        }
        for (rr, cc), pair in choice.items():
            @pl.when((r == rr) & (c == cc))
            def _(pair=pair):
                for h in range(2):
                    for cp in pieces(pair[h], xr, h * width, h):
                        cp.start()
        for h in range(2):
            for cp in pieces(own, xr, h * width, h):
                cp.wait()
        for cp in fixed:
            cp.wait()

        lows = []
        for k in range(NPAN):
            inv = halves(l_ref[slot_of(k, k)])
            row = None
            if k:
                row = halves(
                    jnp.concatenate([l_ref[slot_of(k, j)] for j in range(k)], axis=1)
                )
            lows.append((inv, row))

        def solve(x_ref, at):
            cols = pl.ds(at, WIDE)
            done_h, done_l = [], []
            for k in range(NPAN):
                inv, row = lows[k]
                x = x_ref[pl.ds(k * BLK, BLK), cols]
                if k:
                    x = x - dot3(
                        row,
                        (jnp.concatenate(done_h, axis=0), jnp.concatenate(done_l, axis=0)),
                        1, 0,
                    )
                y = dot3(inv, x, 1, 0)
                x_ref[pl.ds(k * BLK, BLK), cols] = y
                high, low = halves(y)
                done_h.append(high)
                done_l.append(low)

        def loop_r(i, carry):
            solve(xr, pl.multiple_of(i * WIDE, WIDE))
            return carry

        def loop_c(i, carry):
            solve(xc, pl.multiple_of(i * WIDE, WIDE))
            return carry

        lax.fori_loop(0, height // WIDE, loop_r, 0)
        lax.fori_loop(0, width // WIDE, loop_c, 0)

        def clear(x_ref):
            for i in range(NPAN - 1):
                low = (i + 1) * BLK
                x_ref[pl.ds(low, depth - low), pl.ds(i * BLK, BLK)] = jnp.zeros(
                    (depth - low, BLK), f32
                )

        @pl.when(r == 0)
        def _():
            clear(xr)

        @pl.when(c == 0)
        def _():
            clear(xc)

        high, low = halves(xc[...])
        xch[...] = high
        xcl[...] = low

    at = pl.multiple_of(step * TILE, TILE)
    rows = xr[:, pl.ds(at, TILE)].T
    rh, rl = halves(rows)
    mm = lambda a, b: lax.dot_general(
        a, b, (((1,), (0,)), ((), ())), preferred_element_type=f32
    )
    prod = mm(rh, xch[...]) + (mm(rh, xcl[...]) + mm(rl, xch[...]))
    out_ref[...] = -prod

    for t in range(-(-depth // TILE)):
        many = min(TILE, depth - t * TILE)

        @pl.when((r == 0) & (step == t))
        def _(t=t, many=many):
            out_ref[pl.ds(0, many), :] = raw[pl.ds(t * TILE, many), :] + out_ref[pl.ds(0, many), :]

    @pl.when(c == 0)
    def _():
        out_ref[:, pl.ds(0, depth)] = rows


def update(l, sets, R, C, height, width):
    depth = NPAN * BLK
    hbm = pl.BlockSpec(memory_space=pl.ANY)
    return pl.pallas_call(
        functools.partial(update_kernel, R, C, height, width),
        grid=(height // TILE,),
        out_shape=jax.ShapeDtypeStruct((height, width), f32),
        in_specs=[pl.BlockSpec(l.shape, lambda i: (0, 0, 0))] + [hbm] * 12,
        out_specs=pl.BlockSpec((TILE, width), lambda i: (i, 0)),
        scratch_shapes=[
            pltpu.VMEM((depth, height), f32),
            pltpu.VMEM((depth, width), f32),
            pltpu.VMEM((depth, width), f32),
            pltpu.VMEM((depth, width), bf16),
            pltpu.VMEM((depth, width), bf16),
            pltpu.SemaphoreType.DMA((4, 8)),
        ],
    )(l, *[x for pair in sets for x in pair])


def add_kernel(n, order, direct, C, tab, _, *rest):
    arrays = rest[:4]
    out, buf, sin, sout = rest[4:]
    g, r, c = place()
    dev = r * C + c
    kinds = (2, 4) if direct else (4,)

    def each(fn):
        for p, k in enumerate(order):
            def body(i, carry, p=p, k=k):
                s = (g ^ k) * n + i
                for t, kind in enumerate(kinds):
                    a, b = tab[kind, dev, s], tab[kind + 1, dev, s]

                    @pl.when(a >= 0)
                    def _(t=t, a=a, b=b, kind=kind):
                        slot = (t * 4 + p) * n + i
                        there = out.at[pl.ds(pl.multiple_of(a * BLK, BLK), BLK),
                                       pl.ds(pl.multiple_of(b * BLK, BLK), BLK)]
                        fn(arrays[p], i, slot, there, kind)
                return carry
            lax.fori_loop(0, n, body, 0)

    def fetch(arr, i, slot, there, kind):
        pltpu.make_async_copy(there, buf.at[slot], sin.at[slot]).start()

    def combine(arr, i, slot, there, kind):
        pltpu.make_async_copy(there, buf.at[slot], sin.at[slot]).wait()
        x = arr[i]
        buf[slot] = buf[slot] + (x if kind == 2 else x.T)
        pltpu.make_async_copy(buf.at[slot], there, sout.at[slot]).start()

    def finish(arr, i, slot, there, kind):
        pltpu.make_async_copy(buf.at[slot], there, sout.at[slot]).wait()

    each(fetch)
    each(combine)
    each(finish)


def add_blocks(matrix, arrays, tab, order, direct, C):
    n = arrays[0].shape[0]
    total = 4 * n * (2 if direct else 1)
    hbm = pl.BlockSpec(memory_space=pl.ANY)
    vmem = pl.BlockSpec(memory_space=pltpu.VMEM)
    return pl.pallas_call(
        functools.partial(add_kernel, n, order, direct, C),
        out_shape=jax.ShapeDtypeStruct(matrix.shape, f32),
        in_specs=[pl.BlockSpec(memory_space=pltpu.SMEM), hbm] + [vmem] * 4,
        out_specs=hbm,
        input_output_aliases={1: 0},
        scratch_shapes=[
            pltpu.VMEM((total, BLK, BLK), f32),
            pltpu.SemaphoreType.DMA((total,)),
            pltpu.SemaphoreType.DMA((total,)),
        ],
    )(tab, matrix, *arrays)


def fast(normals, transforms, block_map):
    local, hr = normals[0], transforms[0]
    height, width = local.shape
    R, C, G = lax.axis_size("row"), lax.axis_size("col"), lax.axis_size("grp")
    rb, cb = height // BLK, width // BLK
    per = rb // cb
    plan = plan_for(R, C, rb, cb)
    g, r, c = place()

    def among(devices, bit):
        return [
            (gg * R * C + rr * C + cc, (gg ^ bit) * R * C + rr * C + cc)
            for gg in range(G) for rr, cc in devices
        ]

    def along(edges):
        return [
            (gg * R * C + a * C + b, gg * R * C + x * C + y)
            for gg in range(G) for (a, b), (x, y) in edges
        ]

    move = lambda x, perm: lax.ppermute(x, ALL, perm)
    everyone = [(rr, cc) for rr in range(R) for cc in range(C)]
    upper = [(0, cc) for cc in range(C)]
    lower = [(1, cc) for cc in range(C)]

    mine = lax.dynamic_slice_in_dim(hr, (c % per) * cb, cb, 0)
    other = move(mine, along([((cc // per, cc), (1 - cc // per, cc)) for cc in range(C)]))
    hc = jnp.where(r == c // per, mine, other)

    call = functools.partial(transform, local, hr, hc, block_map)

    def parts(n, first):
        second = NEAR ^ FAR ^ first
        return (
            [(2, n, BLK, BLK), (2, n, BLK, BLK)],
            [(1, 0, n, first), (1, 1, n, 3), (0, 0, n, 0), (0, 1, n, second)],
        )

    def shift(groups, by):
        return [(o + by, lead, n, k) for o, lead, n, k in groups]

    ttab = np.zeros((2, R * C, len(plan.T)), np.int32)
    ttab[:, 0] = np.array(plan.T, np.int32).T
    corner = call(
        jnp.asarray(ttab), [(len(plan.T), BLK, BLK)], [(0, None, len(plan.T), None)],
        lambda rr, cc: (rr == 0) & (cc == 0), rb, cb, C,
    )[0]

    firsts = (NEAR, FAR)
    halves_out = []
    for s in range(2):
        stab = np.zeros((2, R * C, 4 * NPAN), np.int32)
        stab[:] = np.array(plan.strips[s], np.int32).T[:, None]
        shapes, groups = parts(NPAN, firsts[s])
        halves_out.append(
            call(jnp.asarray(stab), shapes, groups, lambda rr, cc: rr == 0, rb, cb, C)
        )
    tab_a = plan.owner_tables(plan.A, plan.na)
    tab_b = plan.owner_tables(plan.B, plan.nb)
    shapes, groups = parts(plan.na, FAR)
    out_a = call(jnp.asarray(tab_a), shapes, groups, None, rb, cb, C)
    shapes, groups = parts(plan.nb, NEAR)
    out_b = call(jnp.asarray(tab_b), shapes, groups, lambda rr, cc: rr == 1, rb, cb, C)

    def reduce(keep, send, first, devices):
        second = NEAR ^ FAR ^ first
        got = move(send, among(devices, first))
        onward = keep[1] + got[1]
        last = move(onward, among(devices, second))
        return keep[0] + got[0] + last

    def gather(q, first, devices):
        second = NEAR ^ FAR ^ first
        a = move(q, among(devices, first))
        b = move(q, among(devices, second))
        return [q, a, b, move(a, among(devices, second))], (0, first, second, 3)

    one = [(0, 0)]
    corner = corner + move(corner, among(one, NEAR))
    corner = corner + move(corner, among(one, FAR))
    everywhere = jnp.where(c == 0, corner, 0.0)
    for cc in range(1, C):
        everywhere = everywhere + move(corner, along([((0, 0), (0, cc))]))
    down = along([((0, cc), (1, cc)) for cc in range(C)])
    everywhere = jnp.where(r == 0, everywhere, move(everywhere, down))
    low = factor_all(everywhere)

    order_of = {NEAR: [0, 1, 2, 3], FAR: [0, 2, 1, 3]}
    sets = [[], [], [], [], [], []]
    near = along([((0, 0), (0, 1)), ((0, 1), (0, 0)), ((1, 2), (1, 3)), ((1, 3), (1, 2))])
    over = along([((0, 1), (0, 2)), ((1, 2), (1, 1))])
    end = along([((0, 2), (0, 3)), ((1, 1), (1, 0))])
    for s in range(2):
        keep, send = halves_out[s]
        q = reduce(keep, send, firsts[s], upper)
        got, order = gather(q, firsts[s], upper)
        by_bit = [got[order.index(k)] for k in range(4)]
        strip = jnp.stack(by_bit, axis=0).reshape(4, NPAN * BLK, BLK)
        own = jnp.where(r == 0, strip, move(strip, down))
        swapped = move(own, near)
        b1 = move(own, over)
        b2 = move(swapped, over)
        c1 = move(b1, end)
        c2 = move(b2, end)
        for where, x in zip(sets, (own, swapped, b1, b2, c1, c2)):
            where.append(x)
    matrix = update(low, sets, R, C, height, width)

    q_a = reduce(*out_a, FAR, everyone)
    q_b = reduce(*out_b, NEAR, lower)
    got_a, order_a = gather(q_a, FAR, everyone)
    got_b, order_b = gather(q_b, NEAR, lower)
    pass_a = q_a[: plan.sent]
    e1 = move(pass_a, along(plan.e1))
    e2 = move(jnp.where((r == 0) & (c == 3), pass_a, q_b), along(plan.e2))
    got_1, order_1 = gather(e1, FAR, [d for _, d in plan.e1])
    got_2, order_2 = gather(e2, NEAR, [d for _, d in plan.e2])

    matrix = add_blocks(matrix, got_a, jnp.asarray(tab_a), order_a, True, C)
    matrix = add_blocks(matrix, got_b, jnp.asarray(tab_b), order_b, True, C)
    tab_1 = plan.partner_tables(plan.e1, plan.sent)
    tab_2 = plan.partner_tables(plan.e2, plan.sent)
    matrix = add_blocks(matrix, got_1, jnp.asarray(tab_1), order_1, False, C)
    matrix = add_blocks(matrix, got_2, jnp.asarray(tab_2), order_2, False, C)
    return matrix


def solution(mesh):
    return jax.shard_map(
        fast if fits(mesh) else general,
        mesh=mesh,
        in_specs=(P("grp", "row", "col"), P("grp", "row", None, None), P("grp", None)),
        out_specs=P("row", "col"),
        check_vma=False,
    )
```
